32 devices in a mesh: job: 2 (over y), slab: 16 (over z, x, core).
Axes of the slice: x: 2, y: 2, z: 4, core: 2. Of those that a mesh axis runs over, the one named last changes fastest.
Arguments:
- partials: bfloat16 [8, 32, 256, 256], P('job', None, 'slab'), parts along dimension 0, may hold values from -1.5 to 1.5
- regions: int32 [64, 256, 256], P(('job', 'slab')), parts along dimension 0, may hold values from 0 to 2
- previous: float32 [64, 256, 256], P(('job', 'slab')), parts along dimension 0, may hold values from -6 to 6
Outputs:
- potential: float32 [64, 256, 256], P(('job', 'slab')), parts along dimension 0
The draws below stay inside these ranges and needn't reach their ends.
There are 2 independent parts, one for each index of `job`. The reference program is written for one: setup_inputs(seed, part) draws one part's arguments, and reference() takes and returns one part's arrays. A program takes and returns all parts, laid end to end along the dimension named above; each array names one. Nothing has to cross between parts.
Inputs may be any that keep to these rules, and one draw needn't show every extreme that they name: `regions`: 0 marks the solute's interior, 1 the ion-free solvent layer, 2 bulk solvent.
All inputs are finite; a program needn't handle non-finite values.
Results may differ from the reference program's by a relative error of at most 0.0003.
Values sent between devices are 32-bit elements; how exact they have to be, the bound alone decides.
A program may use at most 256 MiB of HBM per device.

```python
import jax
import jax.numpy as jnp

NXY = 256
BANDS = 4
PRE_SWEEPS = 2
POST_SWEEPS = 2
COARSE_SWEEPS = 4
NZ = 32


def draw_partials(key, part):
    extent = (BANDS, NZ, NXY, NXY)
    values = jnp.clip(0.25 * jax.random.normal(key, extent, jnp.float32), -1.5, 1.5)
    return values.astype(jnp.bfloat16)


def place_ends(values, rng, least, largest):
    longest = values.shape.index(max(values.shape))
    spots = []
    for shift in (0, 1):
        where = [jax.random.randint(jax.random.fold_in(rng, axis), (), 0, length) for axis, length in enumerate(values.shape)]
        where[longest] = (where[longest] + shift) % values.shape[longest]
        spots.append(tuple(where))
    return values.at[spots[0]].set(least).at[spots[1]].set(largest)


def block_scale(key, shape, split, smallest, high):
    def one(dim, parts):
        heights = jax.random.uniform(jax.random.fold_in(jax.random.fold_in(key, 6), dim), (parts,), jnp.float32, smallest / len(split), high / len(split))
        return jnp.repeat(jnp.exp(heights), shape[dim] // parts).reshape((-1,) + (1,) * (len(shape) - dim - 1))

    loudness = one(*split[0])
    for cut in split[1:]:
        loudness = loudness * one(*cut)
    return loudness


def centred(stream_key, shape, scale, limit, cuts=(), held_as=jnp.bfloat16):
    gain = block_scale(stream_key, shape, cuts, -0.22, 0.18) if cuts else 1.0
    values = jax.random.normal(stream_key, shape, jnp.float32) * scale * gain
    return jnp.minimum(jnp.maximum(values, -limit), limit).astype(held_as)


def setup_inputs(seed: int = 0, part: int = 0) -> dict:
    arg_keys = jax.random.split(jax.random.key(seed), 4)
    part_keys = jax.random.split(jax.random.fold_in(arg_keys[3], part), 4)
    partials = draw_partials(jax.random.fold_in(jax.random.fold_in(arg_keys[3], part), 71), part)
    regions = place_ends(jax.random.randint(part_keys[1], (NZ, NXY, NXY), 0, 3), jax.random.fold_in(part_keys[1], 1), 0, 2).astype(jnp.int32)
    previous = centred(part_keys[2], (NZ, NXY, NXY), 1.0, 6.0, ((0, 16),), jnp.float32)
    return {"partials": partials, "regions": regions, "previous": previous}


DAMPING = 0.75
INSIDE = 2.0
SOLVENT = 78.4
SCREEN = 1.4
SOURCE = 16.0 * 3.141592653589793


def pad_whole(values):
    return jnp.pad(values, ((1, 1), (1, 1), (1, 1)))


def shifted_views(padded):
    return (padded[:-2, 1:-1, 1:-1], padded[2:, 1:-1, 1:-1],
            padded[1:-1, :-2, 1:-1], padded[1:-1, 2:, 1:-1],
            padded[1:-1, 1:-1, :-2], padded[1:-1, 1:-1, 2:])


def face_coefficients(padded, spacing_z, spacing_x):
    centre = padded[1:-1, 1:-1, 1:-1]
    spacings = (spacing_z, spacing_z, spacing_x, spacing_x, spacing_x, spacing_x)
    result = []
    for neighbour, spacing in zip(shifted_views(padded), spacings):
        facing = jnp.where(neighbour > 0.0, neighbour, centre)
        result.append(2.0 * centre * facing / ((centre + facing) * spacing))
    return tuple(result)


def diagonal_of(coefficients, screening):
    running = coefficients[0]
    for coefficient in coefficients[1:]:
        running = running + coefficient
    return running + screening


def beside_sum(coefficients, padded):
    neighbours = shifted_views(padded)
    running = coefficients[0] * neighbours[0]
    for position in range(1, 6):
        running = running + coefficients[position] * neighbours[position]
    return running


def remainder(source_term, solution, coefficients, diagonal):
    return source_term - diagonal * solution + beside_sum(coefficients, pad_whole(solution))


def coarsen(values, halve_plane):
    planes = values.shape[0]
    plane_width = values.shape[1]
    if halve_plane:
        blocks = values.reshape(planes // 2, 2, plane_width // 2, 2, plane_width // 2, 2)
        return jnp.mean(blocks, axis=(1, 3, 5))
    return jnp.mean(values.reshape(planes // 2, 2, plane_width, plane_width), axis=1)


def refine(values, halve_plane):
    values = jnp.repeat(values, 2, axis=0)
    if halve_plane:
        values = jnp.repeat(jnp.repeat(values, 2, axis=1), 2, axis=2)
    return values


def v_cycle(source_term, dielectric, screening, initial, spacing_z, spacing_x):
    planes = source_term.shape[0]
    plane_width = source_term.shape[1]
    coefficients = face_coefficients(pad_whole(dielectric), spacing_z, spacing_x)
    diagonal = diagonal_of(coefficients, screening)
    coarsest = planes == 1
    sweeps = COARSE_SWEEPS if coarsest else PRE_SWEEPS
    if initial is None:
        solution = jnp.zeros_like(source_term)
    else:
        solution = initial
    for sweep_index in range(sweeps):
        solution = solution + DAMPING * remainder(source_term, solution, coefficients, diagonal) / diagonal
    if coarsest:
        return solution
    residual = remainder(source_term, solution, coefficients, diagonal)
    halve_plane = plane_width > 1 and plane_width % 2 == 0
    next_x = spacing_x * 4.0 if halve_plane else spacing_x
    correction = v_cycle(coarsen(residual, halve_plane), coarsen(dielectric, halve_plane),
                         coarsen(screening, halve_plane), None, spacing_z * 4.0, next_x)
    solution = solution + refine(correction, halve_plane)
    for sweep_index in range(POST_SWEEPS):
        solution = solution + DAMPING * remainder(source_term, solution, coefficients, diagonal) / diagonal
    return solution


def reference(partials, regions, previous):
    density = jnp.sum(partials, axis=0, dtype=jnp.float32)
    source_term = SOURCE * density
    dielectric = jnp.where(regions == 0, INSIDE, SOLVENT).astype(jnp.float32)
    screening = jnp.where(regions == 2, SCREEN, 0.0).astype(jnp.float32)
    return v_cycle(source_term, dielectric, screening, previous, 1.0, 1.0)
```

```python
import functools

import jax
import jax.numpy as jnp
from jax import lax
from jax.experimental import pallas as pl
from jax.experimental.pallas import tpu as pltpu
from jax.sharding import PartitionSpec as P

PRE_SWEEPS = 2
POST_SWEEPS = 2
COARSE_SWEEPS = 4

DAMPING = 0.75
INSIDE = 2.0
SOLVENT = 78.4
SCREEN = 1.4
SOURCE = 16.0 * 3.141592653589793

F32 = jnp.float32
LANES = 128


def iota(shape, dim):
    return lax.broadcasted_iota(jnp.int32, shape, dim)


def face(mine, other, spacing):
    return mine * other / ((mine + other) * (0.5 * spacing))


def back(v, dim, by=1):
    return pltpu.roll(v, by, dim)


def ahead(v, dim, by=1):
    return pltpu.roll(v, v.shape[dim] - by, dim)


def dot(a, b):
    return lax.dot_general(
        a, b, (((1,), (0,)), ((), ())),
        precision=lax.Precision.HIGHEST, preferred_element_type=F32)


def pool_right(wide, narrow, valid):
    src, dst = iota((wide, narrow), 0), iota((wide, narrow), 1)
    return jnp.where((src // 2 == dst) & (src < valid), 1.0, 0.0).astype(F32)


def pool_left(narrow, wide):
    dst, src = iota((narrow, wide), 0), iota((narrow, wide), 1)
    return jnp.where(src // 2 == dst, 1.0, 0.0).astype(F32)


def spread_right(narrow, wide, valid):
    src, dst = iota((narrow, wide), 0), iota((narrow, wide), 1)
    return jnp.where((dst // 2 == src) & (dst < valid), 1.0, 0.0).astype(F32)


def spread_left(wide, narrow):
    dst, src = iota((wide, narrow), 0), iota((wide, narrow), 1)
    return jnp.where(dst // 2 == src, 1.0, 0.0).astype(F32)


def plane_faces(e, spacing):
    rows, cols = e.shape
    x, y = iota(e.shape, 0), iota(e.shape, 1)
    fx = jnp.where(x > 0, face(e, back(e, 0), spacing), 0.0)
    fy = jnp.where(y > 0, face(e, back(e, 1), spacing), 0.0)
    edges = (jnp.where((x == 0) | (x == rows - 1), 1.0, 0.0)
             + jnp.where((y == 0) | (y == cols - 1), 1.0, 0.0))
    total = fx + ahead(fx, 0) + fy + ahead(fy, 1) + edges * e * (1.0 / spacing)
    return fx, fy, total


def plane_sum(fx, fy, v):
    return fx * back(v, 0) + ahead(fx * v, 0) + fy * back(v, 1) + ahead(fy * v, 1)


def coarse_cycle(b, e, k, planes, nx, sz, sx):
    rows = b.shape[0]
    row, lane = iota(b.shape, 0), iota(b.shape, 1)
    x, z = row % nx, row // nx
    valid = (row < planes * nx) & (lane < nx)
    e = jnp.where(valid, e, 1.0)
    fx = jnp.where(valid & (x > 0), face(e, back(e, 0), sx), 0.0) if nx > 1 else None
    fy = jnp.where(valid & (lane > 0), face(e, back(e, 1), sx), 0.0) if nx > 1 else None
    wrap = nx % rows
    fz = jnp.where(valid & (z > 0), face(e, back(e, 0, wrap), sz), 0.0) if planes > 1 else None
    diag = k + e * (
        (jnp.where(x == 0, 1.0, 0.0) + jnp.where(x == nx - 1, 1.0, 0.0)
         + jnp.where(lane == 0, 1.0, 0.0) + jnp.where(lane == nx - 1, 1.0, 0.0)) * (1.0 / sx)
        + (jnp.where(z == 0, 1.0, 0.0) + jnp.where(z == planes - 1, 1.0, 0.0)) * (1.0 / sz))
    if nx > 1:
        diag = diag + fx + ahead(fx, 0) + fy + ahead(fy, 1)
    if planes > 1:
        diag = diag + fz + ahead(fz, 0, wrap)
    w = jnp.where(valid, DAMPING / jnp.where(valid, diag, 1.0), 0.0)

    def beside(v):
        total = jnp.zeros_like(v)
        if nx > 1:
            total = plane_sum(fx, fy, v)
        if planes > 1:
            total = total + fz * back(v, 0, wrap) + ahead(fz * v, 0, wrap)
        return total

    def sweep(v):
        return (1.0 - DAMPING) * v + w * (b + beside(v))

    v = w * b
    for _ in range((COARSE_SWEEPS if planes == 1 else PRE_SWEEPS) - 1):
        v = sweep(v)
    if planes == 1:
        return v
    r = jnp.where(valid, b - diag * v + beside(v), 0.0)
    halve = nx > 1 and nx % 2 == 0
    nx2 = nx // 2 if halve else nx
    sx2 = sx * 4.0 if halve else sx
    step = planes
    while step * nx > 512 and step % 4 == 0:
        step //= 2
    part = step * nx
    if step == planes:
        part = rows
    real2 = planes // 2 * nx2
    rows2 = max(8, real2)
    part2 = rows2 if step == planes else step // 2 * nx2
    ratio = 2 if halve else 1

    def member(fine, coarse):
        return ((fine < step * nx) & ((fine // nx // 2) * nx2 + fine % nx // ratio == coarse))

    down = jnp.where(member(iota((part2, part), 1), iota((part2, part), 0)), 1.0, 0.0)
    up = jnp.where(member(iota((part, part2), 0), iota((part, part2), 1)), 1.0, 0.0)
    if halve:
        right = pool_right(LANES, LANES, nx)
        left = spread_right(LANES, LANES, nx)
        scale = 0.125
    else:
        scale = 0.5

    def coarsen(f):
        if halve:
            f = dot(f, right)
        parts = [dot(down, f[i:i + part]) for i in range(0, rows, part)]
        return scale * (parts[0] if len(parts) == 1 else jnp.concatenate(parts, axis=0))

    def refine(f):
        if halve:
            f = dot(f, left)
        parts = [dot(up, f[i:i + part2]) for i in range(0, rows2, part2)]
        return parts[0] if len(parts) == 1 else jnp.concatenate(parts, axis=0)

    c = coarse_cycle(coarsen(r), coarsen(jnp.where(valid, e, 0.0)), coarsen(k),
                     planes // 2, nx2, sz * 4.0, sx2)
    v = v + refine(c)
    for _ in range(POST_SWEEPS):
        v = sweep(v)
    return v


REG, V0, V1, V2, V3 = range(5)
E1, A1, A2, A3, A4 = range(5)


def kernel(n, partials, regions, previous, out,
           dens, got, b0, fx0, fy0, fz0, dg0, wt0, halo_reg, halo0, v1, v2, v3,
           halo1, plane1, gb, gk,
           big_send, big_recv, small_send, small_recv, many_send, many_recv, barrier_dummy):
    me = lax.axis_index("slab")
    job = lax.axis_index("job")
    nxy = regions.shape[1]
    half = nxy // 2
    quarter = nxy // 4
    rows = partials.shape[2]
    has_lo, has_hi = me > 0, me < n - 1

    def peer(index):
        return {"slab": index}

    barrier = pltpu.get_barrier_semaphore()

    def greet(off, carry):
        pl.semaphore_signal(barrier, inc=1, device_id=peer(lax.rem(me + off, n)),
                            device_id_type=pl.DeviceIdType.MESH)
        return carry

    lax.fori_loop(1, n, greet, 0)

    @pl.when(jnp.logical_not(has_lo))
    def _():
        for i in range(4):
            halo0[i, 0] = jnp.zeros((nxy, nxy), F32)
        for i in range(5):
            halo1[i, 0] = jnp.zeros((half, half), F32)
        halo_reg[0] = jnp.zeros((nxy, nxy), jnp.int32)

    @pl.when(jnp.logical_not(has_hi))
    def _():
        for i in range(4):
            halo0[i, 1] = jnp.zeros((nxy, nxy), F32)
        for i in range(5):
            halo1[i, 1] = jnp.zeros((half, half), F32)
        halo_reg[1] = jnp.zeros((nxy, nxy), jnp.int32)

    density = partials[0].astype(F32)
    for g in range(1, partials.shape[0]):
        density = density + partials[g].astype(F32)
    dens[...] = (SOURCE * density).reshape(dens.shape)

    pl.semaphore_wait(barrier, n - 1)

    def copies(first, last, dst, sends, recvs, i):
        to_lo = pltpu.make_async_remote_copy(
            src_ref=first, dst_ref=dst.at[1], send_sem=sends.at[i, 0], recv_sem=recvs.at[i, 1],
            device_id=peer(jnp.maximum(me - 1, 0)), device_id_type=pl.DeviceIdType.MESH)
        to_hi = pltpu.make_async_remote_copy(
            src_ref=last, dst_ref=dst.at[0], send_sem=sends.at[i, 1], recv_sem=recvs.at[i, 0],
            device_id=peer(jnp.minimum(me + 1, n - 1)), device_id_type=pl.DeviceIdType.MESH)

        def start():
            pl.when(has_lo)(to_lo.start)
            pl.when(has_hi)(to_hi.start)

        def recv():
            pl.when(has_lo)(to_hi.wait_recv)
            pl.when(has_hi)(to_lo.wait_recv)

        def sent():
            pl.when(has_lo)(to_lo.wait_send)
            pl.when(has_hi)(to_hi.wait_send)

        return start, recv, sent

    pending = []

    def launch(first, last, dst, sends, recvs, i):
        start, recv, sent = copies(first, last, dst, sends, recvs, i)
        start()
        pending.append(sent)
        return recv

    recv_reg = launch(regions.at[0], regions.at[1], halo_reg, big_send, big_recv, REG)
    recv_v0 = launch(previous.at[0], previous.at[1], halo0.at[0], big_send, big_recv, V0)

    def scatter(off, carry):
        other = lax.rem(me + off, n)
        pltpu.make_async_remote_copy(
            src_ref=dens.at[other], dst_ref=got.at[me], send_sem=many_send.at[0],
            recv_sem=many_recv.at[0], device_id=peer(other),
            device_id_type=pl.DeviceIdType.MESH).start()
        return carry

    lax.fori_loop(1, n, scatter, 0)

    def dielectric(r):
        return jnp.where(r == 0, INSIDE, SOLVENT).astype(F32)

    e = [dielectric(regions[p]) for p in range(2)]
    k = [jnp.where(regions[p] == 2, SCREEN, 0.0).astype(F32) for p in range(2)]
    right0, left0 = pool_right(nxy, half, nxy), pool_left(half, nxy)
    right1, left1 = pool_right(half, LANES, half), pool_left(quarter, half)

    def down0(a, b):
        return 0.125 * dot(left0, dot(a + b, right0))

    def down1(a):
        return 0.25 * dot(left1, dot(a, right1))

    e1, k1 = down0(e[0], e[1]), down0(k[0], k[1])
    plane1[E1] = e1
    recv_e1 = launch(plane1.at[E1], plane1.at[E1], halo1.at[E1], small_send, small_recv, E1)
    gk[me, 0] = down1(e1)
    gk[me, 1] = down1(k1)

    def share(ref, i):
        def one(off, carry):
            other = lax.rem(me + off, n)
            pltpu.make_async_remote_copy(
                src_ref=ref.at[me], dst_ref=ref.at[me], send_sem=many_send.at[i],
                recv_sem=many_recv.at[i], device_id=peer(other),
                device_id_type=pl.DeviceIdType.MESH).start()
            return carry

        lax.fori_loop(1, n, one, 0)

    def all_in(ref, sems, i):
        window = ref.at[pl.ds(0, n - 1)]
        pltpu.make_async_copy(window, window, sems.at[i]).wait()

    share(gk, 1)

    recv_reg()
    e_lo = jnp.where(has_lo, dielectric(halo_reg[0]), e[0])
    e_hi = jnp.where(has_hi, dielectric(halo_reg[1]), e[1])
    faces_z = [face(e_lo, e[0], 1.0), face(e[0], e[1], 1.0), face(e[1], e_hi, 1.0)]
    for i in range(3):
        fz0[i] = faces_z[i]
    for p in range(2):
        fx, fy, total = plane_faces(e[p], 1.0)
        fx0[p] = fx
        fy0[p] = fy
        total = total + faces_z[p] + faces_z[p + 1] + k[p]
        dg0[p] = total
        wt0[p] = DAMPING / total

    def beside0(p, mine, below, above):
        return plane_sum(fx0[p], fy0[p], mine) + fz0[p] * below + fz0[p + 1] * above

    recv_e1()
    sz1 = sx1 = 4.0
    fx1, fy1, total1 = plane_faces(e1, sx1)
    fz1lo = face(jnp.where(has_lo, halo1[E1, 0], e1), e1, sz1)
    fz1hi = face(jnp.where(has_hi, halo1[E1, 1], e1), e1, sz1)
    dg1 = total1 + fz1lo + fz1hi + k1
    wt1 = DAMPING / dg1

    def sweep0(p, mine, below, above):
        return (1.0 - DAMPING) * mine + wt0[p] * (b0[p] + beside0(p, mine, below, above))

    recv_v0()
    previous_planes = [previous[0], previous[1]]
    part = [
        (1.0 - DAMPING) * previous_planes[0]
        + wt0[0] * beside0(0, previous_planes[0], halo0[0, 0], previous_planes[1]),
        (1.0 - DAMPING) * previous_planes[1]
        + wt0[1] * beside0(1, previous_planes[1], previous_planes[0], halo0[0, 1])]
    for p in range(2):
        v1[p] = part[p]

    got[me] = dens[me]
    all_in(got, many_recv, 0)
    for p in range(2):
        if rows % 8 == 0:
            b0[p] = got[:, p].reshape(nxy, nxy)
        else:
            for s in range(n):
                b0[p, s * rows:(s + 1) * rows, :] = got[s, p]
    for p in range(2):
        v1[p] = v1[p] + wt0[p] * b0[p]
    recv = launch(v1.at[0], v1.at[1], halo0.at[1], big_send, big_recv, V1)
    recv()
    v2[0] = sweep0(0, v1[0], halo0[1, 0], v1[1])
    v2[1] = sweep0(1, v1[1], v1[0], halo0[1, 1])
    recv = launch(v2.at[0], v2.at[1], halo0.at[2], big_send, big_recv, V2)
    recv()
    r0 = b0[0] - dg0[0] * v2[0] + beside0(0, v2[0], halo0[2, 0], v2[1])
    r1 = b0[1] - dg0[1] * v2[1] + beside0(1, v2[1], v2[0], halo0[2, 1])
    b1 = down0(r0, r1)

    def beside1(mine, i):
        return plane_sum(fx1, fy1, mine) + fz1lo * halo1[i, 0] + fz1hi * halo1[i, 1]

    def trade1(value, i):
        plane1[i] = value
        launch(plane1.at[i], plane1.at[i], halo1.at[i], small_send, small_recv, i)()

    a = wt1 * b1
    trade1(a, A1)
    a = (1.0 - DAMPING) * a + wt1 * (b1 + beside1(a, A1))
    trade1(a, A2)
    gb[me] = down1(b1 - dg1 * a + beside1(a, A2))
    share(gb, 2)
    all_in(gk, many_recv, 1)
    pair = gk[...].reshape(n // 2, 2, 2, quarter, LANES)
    e2 = 0.5 * (pair[:, 0, 0] + pair[:, 1, 0]).reshape(n // 2 * quarter, LANES)
    k2 = 0.5 * (pair[:, 0, 1] + pair[:, 1, 1]).reshape(n // 2 * quarter, LANES)
    all_in(gb, many_recv, 2)
    pair = gb[...].reshape(n // 2, 2, quarter, LANES)
    b2 = 0.5 * (pair[:, 0] + pair[:, 1]).reshape(n // 2 * quarter, LANES)
    c2 = coarse_cycle(b2, e2, k2, n // 2, quarter, 16.0, 16.0)

    for i in range(n // 2):
        dens2 = c2[i * quarter:(i + 1) * quarter]
        barrier_dummy[i] = dens2
    grow_l, grow_r = spread_left(half, quarter), spread_right(LANES, half, half)

    def up1(index):
        return dot(grow_l, dot(barrier_dummy[index // 2], grow_r))

    halo1[A2, 0] = halo1[A2, 0] + jnp.where(has_lo, up1(jnp.maximum(me - 1, 0)), 0.0)
    halo1[A2, 1] = halo1[A2, 1] + jnp.where(has_hi, up1(jnp.minimum(me + 1, n - 1)), 0.0)
    a = a + up1(me)
    a = (1.0 - DAMPING) * a + wt1 * (b1 + beside1(a, A2))
    trade1(a, A3)
    a = (1.0 - DAMPING) * a + wt1 * (b1 + beside1(a, A3))
    trade1(a, A4)

    big_l, big_r = spread_left(nxy, half), spread_right(half, nxy, nxy)

    def up0(c):
        return dot(big_l, dot(c, big_r))

    mine = up0(a)
    below = halo0[2, 0] + up0(halo1[A4, 0])
    above = halo0[2, 1] + up0(halo1[A4, 1])
    w0, w1 = v2[0] + mine, v2[1] + mine
    v3[0] = sweep0(0, w0, below, w1)
    v3[1] = sweep0(1, w1, w0, above)
    recv = launch(v3.at[0], v3.at[1], halo0.at[3], big_send, big_recv, V3)
    recv()
    out[0] = sweep0(0, v3[0], halo0[3, 0], v3[1])
    out[1] = sweep0(1, v3[1], v3[0], halo0[3, 1])

    for sent in pending:
        sent()
    all_in(got, many_send, 0)
    all_in(gk, many_send, 1)
    all_in(gb, many_send, 2)


def local(partials, regions, previous):
    n = lax.axis_size("slab")
    nxy = regions.shape[1]
    half, quarter = nxy // 2, nxy // 4
    rows = partials.shape[2]
    vmem = lambda *shape: pltpu.VMEM(shape, F32)
    spec = pl.BlockSpec(memory_space=pltpu.VMEM)
    return pl.pallas_call(
        functools.partial(kernel, n),
        out_shape=jax.ShapeDtypeStruct(previous.shape, F32),
        in_specs=[spec] * 3,
        out_specs=spec,
        scratch_shapes=[
            vmem(n, 2, rows, nxy), vmem(n, 2, rows, nxy), vmem(2, nxy, nxy),
            vmem(2, nxy, nxy), vmem(2, nxy, nxy), vmem(3, nxy, nxy), vmem(2, nxy, nxy),
            vmem(2, nxy, nxy),
            pltpu.VMEM((2, nxy, nxy), jnp.int32), vmem(4, 2, nxy, nxy),
            vmem(2, nxy, nxy), vmem(2, nxy, nxy), vmem(2, nxy, nxy),
            vmem(5, 2, half, half), vmem(5, half, half),
            vmem(n, quarter, LANES), vmem(n, 2, quarter, LANES),
            pltpu.SemaphoreType.DMA((5, 2)), pltpu.SemaphoreType.DMA((5, 2)),
            pltpu.SemaphoreType.DMA((5, 2)), pltpu.SemaphoreType.DMA((5, 2)),
            pltpu.SemaphoreType.DMA((3,)), pltpu.SemaphoreType.DMA((3,)),
            vmem(n // 2, quarter, LANES),
        ],
        compiler_params=pltpu.CompilerParams(
            collective_id=0, has_side_effects=True, vmem_limit_bytes=60 * 1024 * 1024),
    )(partials, regions, previous)


def solution(mesh):
    in_specs = (
        P("job", None, "slab", None),
        P(("job", "slab"), None, None),
        P(("job", "slab"), None, None),
    )
    out_specs = P(("job", "slab"), None, None)
    return jax.shard_map(local, mesh=mesh, in_specs=in_specs, out_specs=out_specs, check_vma=False)
```

```python
import functools

import jax
import jax.numpy as jnp
from jax import lax
from jax.experimental import pallas as pl
from jax.experimental.pallas import tpu as pltpu
from jax.sharding import PartitionSpec as P

PRE_SWEEPS = 2
POST_SWEEPS = 2
COARSE_SWEEPS = 4

DAMPING = 0.75
INSIDE = 2.0
SOLVENT = 78.4
SCREEN = 1.4
SOURCE = 16.0 * 3.141592653589793

F32 = jnp.float32
LANES = 128


def iota(shape, dim):
    return lax.broadcasted_iota(jnp.int32, shape, dim)


def face(mine, other, spacing):
    return mine * other / ((mine + other) * (0.5 * spacing))


def back(v, dim, by=1):
    return pltpu.roll(v, by, dim)


def ahead(v, dim, by=1):
    return pltpu.roll(v, v.shape[dim] - by, dim)


def dot(a, b):
    return lax.dot_general(
        a, b, (((1,), (0,)), ((), ())),
        precision=lax.Precision.HIGHEST, preferred_element_type=F32)


def pool_right(wide, narrow, valid):
    src, dst = iota((wide, narrow), 0), iota((wide, narrow), 1)
    return jnp.where((src // 2 == dst) & (src < valid), 1.0, 0.0).astype(F32)


def pool_left(narrow, wide):
    dst, src = iota((narrow, wide), 0), iota((narrow, wide), 1)
    return jnp.where(src // 2 == dst, 1.0, 0.0).astype(F32)


def spread_right(narrow, wide, valid):
    src, dst = iota((narrow, wide), 0), iota((narrow, wide), 1)
    return jnp.where((dst // 2 == src) & (dst < valid), 1.0, 0.0).astype(F32)


def spread_left(wide, narrow):
    dst, src = iota((wide, narrow), 0), iota((wide, narrow), 1)
    return jnp.where(dst // 2 == src, 1.0, 0.0).astype(F32)


def plane_faces(e, spacing):
    rows, cols = e.shape
    x, y = iota(e.shape, 0), iota(e.shape, 1)
    fx = jnp.where(x > 0, face(e, back(e, 0), spacing), 0.0)
    fy = jnp.where(y > 0, face(e, back(e, 1), spacing), 0.0)
    edges = (jnp.where((x == 0) | (x == rows - 1), 1.0, 0.0)
             + jnp.where((y == 0) | (y == cols - 1), 1.0, 0.0))
    total = fx + ahead(fx, 0) + fy + ahead(fy, 1) + edges * e * (1.0 / spacing)
    return fx, fy, total


def plane_sum(fx, fy, v):
    return fx * back(v, 0) + ahead(fx * v, 0) + fy * back(v, 1) + ahead(fy * v, 1)


def coarse_cycle(b, e, k, planes, nx, sz, sx):
    rows = b.shape[0]
    row, lane = iota(b.shape, 0), iota(b.shape, 1)
    x, z = row % nx, row // nx
    valid = (row < planes * nx) & (lane < nx)
    e = jnp.where(valid, e, 1.0)
    fx = jnp.where(valid & (x > 0), face(e, back(e, 0), sx), 0.0) if nx > 1 else None
    fy = jnp.where(valid & (lane > 0), face(e, back(e, 1), sx), 0.0) if nx > 1 else None
    wrap = nx % rows
    fz = jnp.where(valid & (z > 0), face(e, back(e, 0, wrap), sz), 0.0) if planes > 1 else None
    diag = k + e * (
        (jnp.where(x == 0, 1.0, 0.0) + jnp.where(x == nx - 1, 1.0, 0.0)
         + jnp.where(lane == 0, 1.0, 0.0) + jnp.where(lane == nx - 1, 1.0, 0.0)) * (1.0 / sx)
        + (jnp.where(z == 0, 1.0, 0.0) + jnp.where(z == planes - 1, 1.0, 0.0)) * (1.0 / sz))
    if nx > 1:
        diag = diag + fx + ahead(fx, 0) + fy + ahead(fy, 1)
    if planes > 1:
        diag = diag + fz + ahead(fz, 0, wrap)
    w = jnp.where(valid, DAMPING / jnp.where(valid, diag, 1.0), 0.0)

    def beside(v):
        total = jnp.zeros_like(v)
        if nx > 1:
            total = plane_sum(fx, fy, v)
        if planes > 1:
            total = total + fz * back(v, 0, wrap) + ahead(fz * v, 0, wrap)
        return total

    def sweep(v):
        return (1.0 - DAMPING) * v + w * (b + beside(v))

    v = w * b
    for _ in range((COARSE_SWEEPS if planes == 1 else PRE_SWEEPS) - 1):
        v = sweep(v)
    if planes == 1:
        return v
    r = jnp.where(valid, b - diag * v + beside(v), 0.0)
    halve = nx > 1 and nx % 2 == 0
    nx2 = nx // 2 if halve else nx
    sx2 = sx * 4.0 if halve else sx
    step = planes
    while step * nx > 512 and step % 4 == 0:
        step //= 2
    part = step * nx
    if step == planes:
        part = rows
    real2 = planes // 2 * nx2
    rows2 = max(8, real2)
    part2 = rows2 if step == planes else step // 2 * nx2
    ratio = 2 if halve else 1

    def member(fine, coarse):
        return ((fine < step * nx) & ((fine // nx // 2) * nx2 + fine % nx // ratio == coarse))

    down = jnp.where(member(iota((part2, part), 1), iota((part2, part), 0)), 1.0, 0.0)
    up = jnp.where(member(iota((part, part2), 0), iota((part, part2), 1)), 1.0, 0.0)
    if halve:
        right = pool_right(LANES, LANES, nx)
        left = spread_right(LANES, LANES, nx)
        scale = 0.125
    else:
        scale = 0.5

    def coarsen(f):
        if halve:
            f = dot(f, right)
        parts = [dot(down, f[i:i + part]) for i in range(0, rows, part)]
        return scale * (parts[0] if len(parts) == 1 else jnp.concatenate(parts, axis=0))

    def refine(f):
        if halve:
            f = dot(f, left)
        parts = [dot(up, f[i:i + part2]) for i in range(0, rows2, part2)]
        return parts[0] if len(parts) == 1 else jnp.concatenate(parts, axis=0)

    c = coarse_cycle(coarsen(r), coarsen(jnp.where(valid, e, 0.0)), coarsen(k),
                     planes // 2, nx2, sz * 4.0, sx2)
    v = v + refine(c)
    for _ in range(POST_SWEEPS):
        v = sweep(v)
    return v


REG, V0, V1, V2, V3 = range(5)
E1, A1, A2, A3, A4, TERM = range(6)


def kernel(n, partials, regions, previous, out,
           dens, got, b0, fx0, fy0, fz0, dg0, wt0, halo_reg, halo0, v1, v2, v3,
           halo1, plane1, term1, gb, gk,
           big_send, big_recv, small_send, small_recv, many_send, many_recv, c2_planes):
    me = lax.axis_index("slab")
    job = lax.axis_index("job")
    nxy = regions.shape[1]
    half = nxy // 2
    quarter = nxy // 4
    rows = partials.shape[2]
    has_lo, has_hi = me > 0, me < n - 1

    def peer(index):
        return {"slab": index}

    barrier = pltpu.get_barrier_semaphore()

    def greet(off, carry):
        pl.semaphore_signal(barrier, inc=1, device_id=peer(lax.rem(me + off, n)),
                            device_id_type=pl.DeviceIdType.MESH)
        return carry

    lax.fori_loop(1, n, greet, 0)

    @pl.when(jnp.logical_not(has_lo))
    def _():
        for i in range(4):
            halo0[i, 0] = jnp.zeros((nxy, nxy), F32)
        for i in range(6):
            halo1[i, 0] = jnp.zeros((half, half), F32)
        halo_reg[0] = jnp.zeros((nxy, nxy), jnp.int32)

    @pl.when(jnp.logical_not(has_hi))
    def _():
        for i in range(4):
            halo0[i, 1] = jnp.zeros((nxy, nxy), F32)
        for i in range(6):
            halo1[i, 1] = jnp.zeros((half, half), F32)
        halo_reg[1] = jnp.zeros((nxy, nxy), jnp.int32)

    density = partials[0].astype(F32)
    for g in range(1, partials.shape[0]):
        density = density + partials[g].astype(F32)
    dens[...] = (SOURCE * density).reshape(dens.shape)

    pl.semaphore_wait(barrier, n - 1)

    def copies(first, last, dst, sends, recvs, i):
        to_lo = pltpu.make_async_remote_copy(
            src_ref=first, dst_ref=dst.at[1], send_sem=sends.at[i, 0], recv_sem=recvs.at[i, 1],
            device_id=peer(jnp.maximum(me - 1, 0)), device_id_type=pl.DeviceIdType.MESH)
        to_hi = pltpu.make_async_remote_copy(
            src_ref=last, dst_ref=dst.at[0], send_sem=sends.at[i, 1], recv_sem=recvs.at[i, 0],
            device_id=peer(jnp.minimum(me + 1, n - 1)), device_id_type=pl.DeviceIdType.MESH)

        def start():
            pl.when(has_lo)(to_lo.start)
            pl.when(has_hi)(to_hi.start)

        def recv():
            pl.when(has_lo)(to_hi.wait_recv)
            pl.when(has_hi)(to_lo.wait_recv)

        def sent():
            pl.when(has_lo)(to_lo.wait_send)
            pl.when(has_hi)(to_hi.wait_send)

        return start, recv, sent

    pending = []

    def launch(first, last, dst, sends, recvs, i):
        start, recv, sent = copies(first, last, dst, sends, recvs, i)
        start()
        pending.append(sent)
        return recv

    recv_reg = launch(regions.at[0], regions.at[1], halo_reg, big_send, big_recv, REG)
    recv_v0 = launch(previous.at[0], previous.at[1], halo0.at[0], big_send, big_recv, V0)

    def scatter(step, carry):
        other = lax.rem(me + 1 + lax.rem(step + n // 2 - 1, n - 1), n)
        pltpu.make_async_remote_copy(
            src_ref=dens.at[other], dst_ref=got.at[me], send_sem=many_send.at[0],
            recv_sem=many_recv.at[0], device_id=peer(other),
            device_id_type=pl.DeviceIdType.MESH).start()
        return carry

    lax.fori_loop(0, n - 1, scatter, 0)

    def dielectric(r):
        return jnp.where(r == 0, INSIDE, SOLVENT).astype(F32)

    e = [dielectric(regions[p]) for p in range(2)]
    k = [jnp.where(regions[p] == 2, SCREEN, 0.0).astype(F32) for p in range(2)]
    right0, left0 = pool_right(nxy, half, nxy), pool_left(half, nxy)
    right1, left1 = pool_right(half, LANES, half), pool_left(quarter, half)

    def down0(a, b):
        return 0.125 * dot(left0, dot(a + b, right0))

    def down1(a):
        return 0.25 * dot(left1, dot(a, right1))

    e1, k1 = down0(e[0], e[1]), down0(k[0], k[1])
    plane1[E1] = e1
    recv_e1 = launch(plane1.at[E1], plane1.at[E1], halo1.at[E1], small_send, small_recv, E1)
    core, chip = lax.rem(me, 2), me // 2
    gk[core, chip] = down1(e1) + back(down1(k1), 1, LANES // 2)

    def share(ref, i):
        def one(off, carry):
            other = lax.rem(me + 2 * off, n)
            pltpu.make_async_remote_copy(
                src_ref=ref.at[core, chip], dst_ref=ref.at[core, chip], send_sem=many_send.at[i],
                recv_sem=many_recv.at[i], device_id=peer(other),
                device_id_type=pl.DeviceIdType.MESH).start()
            return carry

        lax.fori_loop(1, n // 2, one, 0)

    def relay(ref, i):
        window = ref.at[0, pl.ds(0, n // 2 - 1)]
        pltpu.make_async_copy(window, window, many_recv.at[i]).wait()
        copy = pltpu.make_async_remote_copy(
            src_ref=ref.at[core], dst_ref=ref.at[core], send_sem=many_send.at[i + 2],
            recv_sem=many_recv.at[i + 2], device_id=peer(me + 1 - 2 * core),
            device_id_type=pl.DeviceIdType.MESH)
        copy.start()
        pending.append(pltpu.make_async_copy(window, window, many_send.at[i]).wait)
        pending.append(copy.wait_send)
        return copy.wait_recv

    def all_in(ref, sems, i):
        window = ref.at[pl.ds(0, n - 1)]
        pltpu.make_async_copy(window, window, sems.at[i]).wait()

    share(gk, 1)

    recv_reg()
    e_lo = jnp.where(has_lo, dielectric(halo_reg[0]), e[0])
    e_hi = jnp.where(has_hi, dielectric(halo_reg[1]), e[1])
    faces_z = [face(e_lo, e[0], 1.0), face(e[0], e[1], 1.0), face(e[1], e_hi, 1.0)]
    for i in range(3):
        fz0[i] = faces_z[i]
    for p in range(2):
        fx, fy, total = plane_faces(e[p], 1.0)
        fx0[p] = fx
        fy0[p] = fy
        total = total + faces_z[p] + faces_z[p + 1] + k[p]
        dg0[p] = total
        wt0[p] = DAMPING / total

    def beside0(p, mine, below, above):
        return plane_sum(fx0[p], fy0[p], mine) + fz0[p] * below + fz0[p + 1] * above

    recv_e1()
    sz1 = sx1 = 4.0
    fx1, fy1, total1 = plane_faces(e1, sx1)
    fz1lo = face(jnp.where(has_lo, halo1[E1, 0], e1), e1, sz1)
    fz1hi = face(jnp.where(has_hi, halo1[E1, 1], e1), e1, sz1)
    dg1 = total1 + fz1lo + fz1hi + k1
    wt1 = DAMPING / dg1

    def sweep0(p, mine, below, above):
        return (1.0 - DAMPING) * mine + wt0[p] * (b0[p] + beside0(p, mine, below, above))

    recv_v0()
    previous_planes = [previous[0], previous[1]]
    part = [
        (1.0 - DAMPING) * previous_planes[0]
        + wt0[0] * beside0(0, previous_planes[0], halo0[0, 0], previous_planes[1]),
        (1.0 - DAMPING) * previous_planes[1]
        + wt0[1] * beside0(1, previous_planes[1], previous_planes[0], halo0[0, 1])]
    for p in range(2):
        v1[p] = part[p]

    got[me] = dens[me]
    all_in(got, many_recv, 0)
    for p in range(2):
        if rows % 8 == 0:
            b0[p] = got[:, p].reshape(nxy, nxy)
        else:
            for s in range(n):
                b0[p, s * rows:(s + 1) * rows, :] = got[s, p]
    for p in range(2):
        v1[p] = v1[p] + wt0[p] * b0[p]
    recv = launch(v1.at[0], v1.at[1], halo0.at[1], big_send, big_recv, V1)
    recv()
    v2[0] = sweep0(0, v1[0], halo0[1, 0], v1[1])
    v2[1] = sweep0(1, v1[1], v1[0], halo0[1, 1])
    term1[0] = 0.125 * dot(left0, dot(fz0[0] * v2[0], right0))
    term1[1] = 0.125 * dot(left0, dot(fz0[2] * v2[1], right0))
    recv_term = launch(term1.at[0], term1.at[1], halo1.at[TERM], small_send, small_recv, TERM)
    recv_v2 = launch(v2.at[0], v2.at[1], halo0.at[2], big_send, big_recv, V2)
    r0 = b0[0] - dg0[0] * v2[0] + plane_sum(fx0[0], fy0[0], v2[0]) + fz0[1] * v2[1]
    r1 = b0[1] - dg0[1] * v2[1] + plane_sum(fx0[1], fy0[1], v2[1]) + fz0[1] * v2[0]
    b1 = down0(r0, r1)
    recv_gk = relay(gk, 1)
    recv_term()
    b1 = b1 + halo1[TERM, 0] + halo1[TERM, 1]

    def beside1(mine, i):
        return plane_sum(fx1, fy1, mine) + fz1lo * halo1[i, 0] + fz1hi * halo1[i, 1]

    def trade1(value, i):
        plane1[i] = value
        launch(plane1.at[i], plane1.at[i], halo1.at[i], small_send, small_recv, i)()

    a = wt1 * b1
    trade1(a, A1)
    a = (1.0 - DAMPING) * a + wt1 * (b1 + beside1(a, A1))
    trade1(a, A2)
    full = down1(b1 - dg1 * a + beside1(a, A2))
    gb[core, chip] = full[:quarter // 2] + back(full[quarter // 2:], 1, LANES // 2)
    share(gb, 2)
    recv_gk()
    e2 = 0.5 * (gk[0] + gk[1]).reshape(n // 2 * quarter, LANES)
    k2 = back(e2, 1, LANES // 2)
    relay(gb, 2)()
    packed = 0.5 * (gb[0] + gb[1]).reshape(n // 2 * quarter // 2, LANES)
    split = (n // 2, quarter // 2, LANES)
    b2 = jnp.concatenate(
        [packed.reshape(split), back(packed, 1, LANES // 2).reshape(split)], axis=1
    ).reshape(n // 2 * quarter, LANES)
    c2 = coarse_cycle(b2, e2, k2, n // 2, quarter, 16.0, 16.0)

    for i in range(n // 2):
        c2_planes[i] = c2[i * quarter:(i + 1) * quarter]
    grow_l, grow_r = spread_left(half, quarter), spread_right(LANES, half, half)

    def up1(index):
        return dot(grow_l, dot(c2_planes[index // 2], grow_r))

    halo1[A2, 0] = halo1[A2, 0] + jnp.where(has_lo, up1(jnp.maximum(me - 1, 0)), 0.0)
    halo1[A2, 1] = halo1[A2, 1] + jnp.where(has_hi, up1(jnp.minimum(me + 1, n - 1)), 0.0)
    a = a + up1(me)
    a = (1.0 - DAMPING) * a + wt1 * (b1 + beside1(a, A2))
    trade1(a, A3)
    a = (1.0 - DAMPING) * a + wt1 * (b1 + beside1(a, A3))
    trade1(a, A4)

    big_l, big_r = spread_left(nxy, half), spread_right(half, nxy, nxy)

    def up0(c):
        return dot(big_l, dot(c, big_r))

    recv_v2()
    mine = up0(a)
    below = halo0[2, 0] + up0(halo1[A4, 0])
    above = halo0[2, 1] + up0(halo1[A4, 1])
    w0, w1 = v2[0] + mine, v2[1] + mine
    v3[0] = sweep0(0, w0, below, w1)
    v3[1] = sweep0(1, w1, w0, above)
    recv = launch(v3.at[0], v3.at[1], halo0.at[3], big_send, big_recv, V3)
    recv()
    out[0] = sweep0(0, v3[0], halo0[3, 0], v3[1])
    out[1] = sweep0(1, v3[1], v3[0], halo0[3, 1])

    for sent in pending:
        sent()
    all_in(got, many_send, 0)


def local(partials, regions, previous):
    n = lax.axis_size("slab")
    nxy = regions.shape[1]
    half, quarter = nxy // 2, nxy // 4
    rows = partials.shape[2]
    vmem = lambda *shape: pltpu.VMEM(shape, F32)
    spec = pl.BlockSpec(memory_space=pltpu.VMEM)
    return pl.pallas_call(
        functools.partial(kernel, n),
        out_shape=jax.ShapeDtypeStruct(previous.shape, F32),
        in_specs=[spec] * 3,
        out_specs=spec,
        scratch_shapes=[
            vmem(n, 2, rows, nxy), vmem(n, 2, rows, nxy), vmem(2, nxy, nxy),
            vmem(2, nxy, nxy), vmem(2, nxy, nxy), vmem(3, nxy, nxy), vmem(2, nxy, nxy),
            vmem(2, nxy, nxy),
            pltpu.VMEM((2, nxy, nxy), jnp.int32), vmem(4, 2, nxy, nxy),
            vmem(2, nxy, nxy), vmem(2, nxy, nxy), vmem(2, nxy, nxy),
            vmem(6, 2, half, half), vmem(5, half, half), vmem(2, half, half),
            vmem(2, n // 2, quarter // 2, LANES), vmem(2, n // 2, quarter, LANES),
            pltpu.SemaphoreType.DMA((5, 2)), pltpu.SemaphoreType.DMA((5, 2)),
            pltpu.SemaphoreType.DMA((6, 2)), pltpu.SemaphoreType.DMA((6, 2)),
            pltpu.SemaphoreType.DMA((5,)), pltpu.SemaphoreType.DMA((5,)),
            vmem(n // 2, quarter, LANES),
        ],
        compiler_params=pltpu.CompilerParams(
            collective_id=0, has_side_effects=True, vmem_limit_bytes=60 * 1024 * 1024),
    )(partials, regions, previous)


def solution(mesh):
    in_specs = (
        P("job", None, "slab", None),
        P(("job", "slab"), None, None),
        P(("job", "slab"), None, None),
    )
    out_specs = P(("job", "slab"), None, None)
    return jax.shard_map(local, mesh=mesh, in_specs=in_specs, out_specs=out_specs, check_vma=False)
```

```python
import functools

import jax
import jax.numpy as jnp
from jax import lax
from jax.experimental import pallas as pl
from jax.experimental.pallas import tpu as pltpu
from jax.sharding import PartitionSpec as P

PRE_SWEEPS = 2
POST_SWEEPS = 2
COARSE_SWEEPS = 4

DAMPING = 0.75
INSIDE = 2.0
SOLVENT = 78.4
SCREEN = 1.4
SOURCE = 16.0 * 3.141592653589793

F32 = jnp.float32
LANES = 128


def iota(shape, dim):
    return lax.broadcasted_iota(jnp.int32, shape, dim)


def face(mine, other, spacing):
    return mine * other / ((mine + other) * (0.5 * spacing))


def back(v, dim, by=1):
    return pltpu.roll(v, by, dim)


def ahead(v, dim, by=1):
    return pltpu.roll(v, v.shape[dim] - by, dim)


def dot(a, b):
    return lax.dot_general(
        a, b, (((1,), (0,)), ((), ())),
        precision=lax.Precision.HIGHEST, preferred_element_type=F32)


def pool_right(wide, narrow, valid):
    src, dst = iota((wide, narrow), 0), iota((wide, narrow), 1)
    return jnp.where((src // 2 == dst) & (src < valid), 1.0, 0.0).astype(F32)


def pool_left(narrow, wide):
    dst, src = iota((narrow, wide), 0), iota((narrow, wide), 1)
    return jnp.where(src // 2 == dst, 1.0, 0.0).astype(F32)


def spread_right(narrow, wide, valid):
    src, dst = iota((narrow, wide), 0), iota((narrow, wide), 1)
    return jnp.where((dst // 2 == src) & (dst < valid), 1.0, 0.0).astype(F32)


def spread_left(wide, narrow):
    dst, src = iota((wide, narrow), 0), iota((wide, narrow), 1)
    return jnp.where(dst // 2 == src, 1.0, 0.0).astype(F32)


def plane_faces(e, spacing):
    rows, cols = e.shape
    x, y = iota(e.shape, 0), iota(e.shape, 1)
    fx = jnp.where(x > 0, face(e, back(e, 0), spacing), 0.0)
    fy = jnp.where(y > 0, face(e, back(e, 1), spacing), 0.0)
    edges = (jnp.where((x == 0) | (x == rows - 1), 1.0, 0.0)
             + jnp.where((y == 0) | (y == cols - 1), 1.0, 0.0))
    total = fx + ahead(fx, 0) + fy + ahead(fy, 1) + edges * e * (1.0 / spacing)
    return fx, fy, total


def plane_sum(fx, fy, v):
    return fx * back(v, 0) + ahead(fx * v, 0) + fy * back(v, 1) + ahead(fy * v, 1)


def coarse_cycle(e, k, planes, nx, sz, sx):
    rows = e.shape[0]
    row, lane = iota(e.shape, 0), iota(e.shape, 1)
    x, z = row % nx, row // nx
    valid = (row < planes * nx) & (lane < nx)
    e = jnp.where(valid, e, 1.0)
    fx = jnp.where(valid & (x > 0), face(e, back(e, 0), sx), 0.0) if nx > 1 else None
    fy = jnp.where(valid & (lane > 0), face(e, back(e, 1), sx), 0.0) if nx > 1 else None
    wrap = nx % rows
    fz = jnp.where(valid & (z > 0), face(e, back(e, 0, wrap), sz), 0.0) if planes > 1 else None
    diag = k + e * (
        (jnp.where(x == 0, 1.0, 0.0) + jnp.where(x == nx - 1, 1.0, 0.0)
         + jnp.where(lane == 0, 1.0, 0.0) + jnp.where(lane == nx - 1, 1.0, 0.0)) * (1.0 / sx)
        + (jnp.where(z == 0, 1.0, 0.0) + jnp.where(z == planes - 1, 1.0, 0.0)) * (1.0 / sz))
    if nx > 1:
        diag = diag + fx + ahead(fx, 0) + fy + ahead(fy, 1)
    if planes > 1:
        diag = diag + fz + ahead(fz, 0, wrap)
    w = jnp.where(valid, DAMPING / jnp.where(valid, diag, 1.0), 0.0)

    def beside(v):
        total = jnp.zeros_like(v)
        if nx > 1:
            total = plane_sum(fx, fy, v)
        if planes > 1:
            total = total + fz * back(v, 0, wrap) + ahead(fz * v, 0, wrap)
        return total

    def sweep(v, b):
        return (1.0 - DAMPING) * v + w * (b + beside(v))

    def coarsest(b):
        v = w * b
        for _ in range(COARSE_SWEEPS - 1):
            v = sweep(v, b)
        return v

    if planes == 1:
        return coarsest
    halve = nx > 1 and nx % 2 == 0
    nx2 = nx // 2 if halve else nx
    sx2 = sx * 4.0 if halve else sx
    step = planes
    while step * nx > 512 and step % 4 == 0:
        step //= 2
    part = step * nx
    if step == planes:
        part = rows
    real2 = planes // 2 * nx2
    rows2 = max(8, real2)
    part2 = rows2 if step == planes else step // 2 * nx2
    ratio = 2 if halve else 1

    def member(fine, coarse):
        return ((fine < step * nx) & ((fine // nx // 2) * nx2 + fine % nx // ratio == coarse))

    down = jnp.where(member(iota((part2, part), 1), iota((part2, part), 0)), 1.0, 0.0)
    up = jnp.where(member(iota((part, part2), 0), iota((part, part2), 1)), 1.0, 0.0)
    if halve:
        right = pool_right(LANES, LANES, nx)
        left = spread_right(LANES, LANES, nx)
        scale = 0.125
    else:
        scale = 0.5

    def coarsen(f):
        if halve:
            f = dot(f, right)
        parts = [dot(down, f[i:i + part]) for i in range(0, rows, part)]
        return scale * (parts[0] if len(parts) == 1 else jnp.concatenate(parts, axis=0))

    def refine(f):
        if halve:
            f = dot(f, left)
        parts = [dot(up, f[i:i + part2]) for i in range(0, rows2, part2)]
        return parts[0] if len(parts) == 1 else jnp.concatenate(parts, axis=0)

    below = coarse_cycle(coarsen(jnp.where(valid, e, 0.0)), coarsen(k),
                         planes // 2, nx2, sz * 4.0, sx2)

    def run(b):
        v = w * b
        for _ in range(PRE_SWEEPS - 1):
            v = sweep(v, b)
        r = jnp.where(valid, b - diag * v + beside(v), 0.0)
        v = v + refine(below(coarsen(r)))
        for _ in range(POST_SWEEPS):
            v = sweep(v, b)
        return v

    return run


REG, V0, V1, V2, BASE, FAR = range(6)
E1, A1, A2, A3, A4, TERM = range(6)


def kernel(n, partials, regions, previous, out,
           dens, got, b0, fx0, fy0, fz0, dg0, wt0, halo_reg, far_reg, fxh, fyh, fzh, wth, halo0, v1, v2, base,
           halo1, plane1, term1, gb, gk,
           big_send, big_recv, small_send, small_recv, many_send, many_recv, c2_planes):
    me = lax.axis_index("slab")
    job = lax.axis_index("job")
    nxy = regions.shape[1]
    half = nxy // 2
    quarter = nxy // 4
    rows = partials.shape[2]
    has_lo, has_hi = me > 0, me < n - 1

    def peer(index):
        return {"slab": index}

    barrier = pltpu.get_barrier_semaphore()

    def greet(off, carry):
        pl.semaphore_signal(barrier, inc=1, device_id=peer(lax.rem(me + off, n)),
                            device_id_type=pl.DeviceIdType.MESH)
        return carry

    lax.fori_loop(1, n, greet, 0)

    @pl.when(jnp.logical_not(has_lo))
    def _():
        for i in range(4):
            halo0[i, 0] = jnp.zeros((nxy, nxy), F32)
        for i in range(6):
            halo1[i, 0] = jnp.zeros((half, half), F32)
        halo_reg[0] = jnp.zeros((nxy, nxy), jnp.int32)
        far_reg[0] = jnp.zeros((nxy, nxy), jnp.int32)

    @pl.when(jnp.logical_not(has_hi))
    def _():
        for i in range(4):
            halo0[i, 1] = jnp.zeros((nxy, nxy), F32)
        for i in range(6):
            halo1[i, 1] = jnp.zeros((half, half), F32)
        halo_reg[1] = jnp.zeros((nxy, nxy), jnp.int32)
        far_reg[1] = jnp.zeros((nxy, nxy), jnp.int32)

    density = partials[0].astype(F32)
    for g in range(1, partials.shape[0]):
        density = density + partials[g].astype(F32)
    dens[...] = (SOURCE * density).reshape(dens.shape)

    pl.semaphore_wait(barrier, n - 1)

    def copies(first, last, dst, sends, recvs, i):
        to_lo = pltpu.make_async_remote_copy(
            src_ref=first, dst_ref=dst.at[1], send_sem=sends.at[i, 0], recv_sem=recvs.at[i, 1],
            device_id=peer(jnp.maximum(me - 1, 0)), device_id_type=pl.DeviceIdType.MESH)
        to_hi = pltpu.make_async_remote_copy(
            src_ref=last, dst_ref=dst.at[0], send_sem=sends.at[i, 1], recv_sem=recvs.at[i, 0],
            device_id=peer(jnp.minimum(me + 1, n - 1)), device_id_type=pl.DeviceIdType.MESH)

        def start():
            pl.when(has_lo)(to_lo.start)
            pl.when(has_hi)(to_hi.start)

        def recv():
            pl.when(has_lo)(to_hi.wait_recv)
            pl.when(has_hi)(to_lo.wait_recv)

        def sent():
            pl.when(has_lo)(to_lo.wait_send)
            pl.when(has_hi)(to_hi.wait_send)

        return start, recv, sent

    pending = []

    def launch(first, last, dst, sends, recvs, i):
        start, recv, sent = copies(first, last, dst, sends, recvs, i)
        start()
        pending.append(sent)
        return recv

    recv_reg = launch(regions.at[0], regions.at[1], halo_reg, big_send, big_recv, REG)
    recv_v0 = launch(previous.at[0], previous.at[1], halo0.at[0], big_send, big_recv, V0)

    def scatter(step, carry):
        other = lax.rem(me + 1 + lax.rem(step + n // 2 - 1, n - 1), n)
        pltpu.make_async_remote_copy(
            src_ref=dens.at[other], dst_ref=got.at[me], send_sem=many_send.at[0],
            recv_sem=many_recv.at[0], device_id=peer(other),
            device_id_type=pl.DeviceIdType.MESH).start()
        return carry

    lax.fori_loop(0, n - 1, scatter, 0)

    def dielectric(r):
        return jnp.where(r == 0, INSIDE, SOLVENT).astype(F32)

    e = [dielectric(regions[p]) for p in range(2)]
    k = [jnp.where(regions[p] == 2, SCREEN, 0.0).astype(F32) for p in range(2)]
    right0, left0 = pool_right(nxy, half, nxy), pool_left(half, nxy)
    right1, left1 = pool_right(half, LANES, half), pool_left(quarter, half)

    def down0(a, b):
        return 0.125 * dot(left0, dot(a + b, right0))

    def down1(a):
        return 0.25 * dot(left1, dot(a, right1))

    e1, k1 = down0(e[0], e[1]), down0(k[0], k[1])
    plane1[E1] = e1
    recv_e1 = launch(plane1.at[E1], plane1.at[E1], halo1.at[E1], small_send, small_recv, E1)
    core, chip = lax.rem(me, 2), me // 2
    gk[core, chip] = down1(e1) + back(down1(k1), 1, LANES // 2)

    def share(ref, i):
        def one(off, carry):
            other = lax.rem(me + 2 * off, n)
            pltpu.make_async_remote_copy(
                src_ref=ref.at[core, chip], dst_ref=ref.at[core, chip], send_sem=many_send.at[i],
                recv_sem=many_recv.at[i], device_id=peer(other),
                device_id_type=pl.DeviceIdType.MESH).start()
            return carry

        lax.fori_loop(1, n // 2, one, 0)

    def relay(ref, i):
        window = ref.at[0, pl.ds(0, n // 2 - 1)]
        pltpu.make_async_copy(window, window, many_recv.at[i]).wait()
        copy = pltpu.make_async_remote_copy(
            src_ref=ref.at[core], dst_ref=ref.at[core], send_sem=many_send.at[i + 2],
            recv_sem=many_recv.at[i + 2], device_id=peer(me + 1 - 2 * core),
            device_id_type=pl.DeviceIdType.MESH)
        copy.start()
        pending.append(pltpu.make_async_copy(window, window, many_send.at[i]).wait)
        pending.append(copy.wait_send)
        return copy.wait_recv

    def all_in(ref, sems, i):
        window = ref.at[pl.ds(0, n - 1)]
        pltpu.make_async_copy(window, window, sems.at[i]).wait()

    share(gk, 1)

    totals = []
    middle = face(e[0], e[1], 1.0)
    fz0[1] = middle
    part = []
    for p in range(2):
        fx, fy, total = plane_faces(e[p], 1.0)
        fx0[p] = fx
        fy0[p] = fy
        totals.append(total + middle + k[p])
        part.append(plane_sum(fx, fy, previous[p]) + middle * previous[1 - p])
    recv_reg()
    e_side = [jnp.where(has_lo, dielectric(halo_reg[0]), e[0]),
              jnp.where(has_hi, dielectric(halo_reg[1]), e[1])]
    for p in range(2):
        outer = face(e_side[p], e[p], 1.0)
        fz0[2 * p] = outer
        total = totals[p] + outer
        dg0[p] = total
        wt0[p] = DAMPING / total

    def beside0(p, mine, below, above):
        return plane_sum(fx0[p], fy0[p], mine) + fz0[p] * below + fz0[p + 1] * above

    def sweep0(p, mine, below, above):
        return (1.0 - DAMPING) * mine + wt0[p] * (b0[p] + beside0(p, mine, below, above))

    recv_v0()
    for p in range(2):
        v1[p] = (1.0 - DAMPING) * previous[p] + wt0[p] * (part[p] + fz0[2 * p] * halo0[0, p])

    got[me] = dens[me]
    all_in(got, many_recv, 0)
    for p in range(2):
        if rows % 8 == 0:
            b0[p] = got[:, p].reshape(nxy, nxy)
        else:
            for s in range(n):
                b0[p, s * rows:(s + 1) * rows, :] = got[s, p]
    for p in range(2):
        v1[p] = v1[p] + wt0[p] * b0[p]
    recv = launch(v1.at[0], v1.at[1], halo0.at[1], big_send, big_recv, V1)
    recv_gk = relay(gk, 1)
    recv_e1()
    sz1 = sx1 = 4.0
    fx1, fy1, total1 = plane_faces(e1, sx1)
    fz1lo = face(jnp.where(has_lo, halo1[E1, 0], e1), e1, sz1)
    fz1hi = face(jnp.where(has_hi, halo1[E1, 1], e1), e1, sz1)
    dg1 = total1 + fz1lo + fz1hi + k1
    wt1 = DAMPING / dg1

    recv()
    v2[0] = sweep0(0, v1[0], halo0[1, 0], v1[1])
    v2[1] = sweep0(1, v1[1], v1[0], halo0[1, 1])
    term1[0] = 0.125 * dot(left0, dot(fz0[0] * v2[0], right0))
    term1[1] = 0.125 * dot(left0, dot(fz0[2] * v2[1], right0))
    recv_term = launch(term1.at[0], term1.at[1], halo1.at[TERM], small_send, small_recv, TERM)
    recv_v2 = launch(v2.at[0], v2.at[1], halo0.at[2], big_send, big_recv, V2)
    r0 = b0[0] - dg0[0] * v2[0] + plane_sum(fx0[0], fy0[0], v2[0]) + fz0[1] * v2[1]
    r1 = b0[1] - dg0[1] * v2[1] + plane_sum(fx0[1], fy0[1], v2[1]) + fz0[1] * v2[0]
    b1 = down0(r0, r1)
    recv_far = launch(regions.at[1], regions.at[0], far_reg, big_send, big_recv, FAR)
    recv_gk()
    e2 = 0.5 * (gk[0] + gk[1]).reshape(n // 2 * quarter, LANES)
    k2 = back(e2, 1, LANES // 2)
    coarse = coarse_cycle(e2, k2, n // 2, quarter, 16.0, 16.0)
    recv_term()
    b1 = b1 + halo1[TERM, 0] + halo1[TERM, 1]

    def beside1(mine, i):
        return plane_sum(fx1, fy1, mine) + fz1lo * halo1[i, 0] + fz1hi * halo1[i, 1]

    def trade1(value, i):
        plane1[i] = value
        launch(plane1.at[i], plane1.at[i], halo1.at[i], small_send, small_recv, i)()

    a = wt1 * b1
    trade1(a, A1)
    a = (1.0 - DAMPING) * a + wt1 * (b1 + beside1(a, A1))
    trade1(a, A2)
    full = down1(b1 - dg1 * a + beside1(a, A2))
    gb[core, chip] = full[:quarter // 2] + back(full[quarter // 2:], 1, LANES // 2)
    share(gb, 2)
    recv_v2()
    base[0] = sweep0(0, v2[0], halo0[2, 0], v2[1])
    base[1] = sweep0(1, v2[1], v2[0], halo0[2, 1])
    recv_base = launch(base.at[0], base.at[1], halo0.at[3], big_send, big_recv, BASE)
    relay_gb = relay(gb, 2)
    recv_far()
    for p in range(2):
        region = halo_reg[p]
        beyond = face(e_side[p], dielectric(far_reg[p]), 1.0)
        fx, fy, total = plane_faces(e_side[p], 1.0)
        fxh[p] = fx
        fyh[p] = fy
        fzh[p] = beyond
        wth[p] = DAMPING / (total + beyond + fz0[2 * p] + jnp.where(region == 2, SCREEN, 0.0))
    relay_gb()
    packed = 0.5 * (gb[0] + gb[1]).reshape(n // 2 * quarter // 2, LANES)
    split = (n // 2, quarter // 2, LANES)
    b2 = jnp.concatenate(
        [packed.reshape(split), back(packed, 1, LANES // 2).reshape(split)], axis=1
    ).reshape(n // 2 * quarter, LANES)
    c2 = coarse(b2)

    for i in range(n // 2):
        c2_planes[i] = c2[i * quarter:(i + 1) * quarter]
    grow_l, grow_r = spread_left(half, quarter), spread_right(LANES, half, half)

    def up1(index):
        return dot(grow_l, dot(c2_planes[index // 2], grow_r))

    halo1[A2, 0] = halo1[A2, 0] + jnp.where(has_lo, up1(jnp.maximum(me - 1, 0)), 0.0)
    halo1[A2, 1] = halo1[A2, 1] + jnp.where(has_hi, up1(jnp.minimum(me + 1, n - 1)), 0.0)
    a = a + up1(me)
    a = (1.0 - DAMPING) * a + wt1 * (b1 + beside1(a, A2))
    trade1(a, A3)
    a = (1.0 - DAMPING) * a + wt1 * (b1 + beside1(a, A3))
    trade1(a, A4)

    big_l, big_r = spread_left(nxy, half), spread_right(half, nxy, nxy)

    def up0(c):
        return dot(big_l, dot(c, big_r))

    mine = up0(a)
    recv_base()
    v3, side = [], []
    present = [has_lo, has_hi]
    for p in range(2):
        c = up0(halo1[A4, p])
        own = plane_sum(fx0[p], fy0[p], mine) + fz0[1] * mine + fz0[2 * p] * c
        v3.append(base[p] + (1.0 - DAMPING) * mine + wt0[p] * own)
        other = plane_sum(fxh[p], fyh[p], c) + fzh[p] * c + fz0[2 * p] * mine
        swept = halo0[3, p] + (1.0 - DAMPING) * c + wth[p] * other
        side.append(jnp.where(present[p], swept, 0.0))
    out[0] = sweep0(0, v3[0], side[0], v3[1])
    out[1] = sweep0(1, v3[1], v3[0], side[1])

    for sent in pending:
        sent()
    all_in(got, many_send, 0)


def local(partials, regions, previous):
    n = lax.axis_size("slab")
    nxy = regions.shape[1]
    half, quarter = nxy // 2, nxy // 4
    rows = partials.shape[2]
    vmem = lambda *shape: pltpu.VMEM(shape, F32)
    spec = pl.BlockSpec(memory_space=pltpu.VMEM)
    return pl.pallas_call(
        functools.partial(kernel, n),
        out_shape=jax.ShapeDtypeStruct(previous.shape, F32),
        in_specs=[spec] * 3,
        out_specs=spec,
        scratch_shapes=[
            vmem(n, 2, rows, nxy), vmem(n, 2, rows, nxy), vmem(2, nxy, nxy),
            vmem(2, nxy, nxy), vmem(2, nxy, nxy), vmem(3, nxy, nxy), vmem(2, nxy, nxy),
            vmem(2, nxy, nxy),
            pltpu.VMEM((2, nxy, nxy), jnp.int32), pltpu.VMEM((2, nxy, nxy), jnp.int32),
            vmem(2, nxy, nxy), vmem(2, nxy, nxy), vmem(2, nxy, nxy), vmem(2, nxy, nxy),
            vmem(4, 2, nxy, nxy),
            vmem(2, nxy, nxy), vmem(2, nxy, nxy), vmem(2, nxy, nxy),
            vmem(6, 2, half, half), vmem(5, half, half), vmem(2, half, half),
            vmem(2, n // 2, quarter // 2, LANES), vmem(2, n // 2, quarter, LANES),
            pltpu.SemaphoreType.DMA((6, 2)), pltpu.SemaphoreType.DMA((6, 2)),
            pltpu.SemaphoreType.DMA((6, 2)), pltpu.SemaphoreType.DMA((6, 2)),
            pltpu.SemaphoreType.DMA((5,)), pltpu.SemaphoreType.DMA((5,)),
            vmem(n // 2, quarter, LANES),
        ],
        compiler_params=pltpu.CompilerParams(
            collective_id=0, has_side_effects=True, vmem_limit_bytes=60 * 1024 * 1024),
    )(partials, regions, previous)


def solution(mesh):
    in_specs = (
        P("job", None, "slab", None),
        P(("job", "slab"), None, None),
        P(("job", "slab"), None, None),
    )
    out_specs = P(("job", "slab"), None, None)
    return jax.shard_map(local, mesh=mesh, in_specs=in_specs, out_specs=out_specs, check_vma=False)
```

```python
import functools

import jax
import jax.numpy as jnp
from jax import lax
from jax.experimental import pallas as pl
from jax.experimental.pallas import tpu as pltpu
from jax.sharding import PartitionSpec as P

PRE_SWEEPS = 2
POST_SWEEPS = 2
COARSE_SWEEPS = 4

DAMPING = 0.75
INSIDE = 2.0
SOLVENT = 78.4
SCREEN = 1.4
SOURCE = 16.0 * 3.141592653589793

F32 = jnp.float32
LANES = 128


def iota(shape, dim):
    return lax.broadcasted_iota(jnp.int32, shape, dim)


def face(mine, other, spacing):
    return mine * other / ((mine + other) * (0.5 * spacing))


def back(v, dim, by=1):
    return pltpu.roll(v, by, dim)


def ahead(v, dim, by=1):
    return pltpu.roll(v, v.shape[dim] - by, dim)


def terms(v):
    result = []
    for _ in range(3):
        result.append(v.astype(jnp.bfloat16))
        v = v - result[-1].astype(F32)
    return result


def product(a, b):
    return lax.dot_general(a, b, (((1,), (0,)), ((), ())), preferred_element_type=F32)


def times(v, selector):
    high, middle, low = (product(t, selector.astype(jnp.bfloat16)) for t in terms(v))
    return high + (middle + low)


def dot(selector, v):
    high, middle, low = (product(selector.astype(jnp.bfloat16), t) for t in terms(v))
    return high + (middle + low)


def pool_right(wide, narrow, valid):
    src, dst = iota((wide, narrow), 0), iota((wide, narrow), 1)
    return jnp.where((src // 2 == dst) & (src < valid), 1.0, 0.0).astype(F32)


def pool_left(narrow, wide):
    dst, src = iota((narrow, wide), 0), iota((narrow, wide), 1)
    return jnp.where(src // 2 == dst, 1.0, 0.0).astype(F32)


def spread_right(narrow, wide, valid):
    src, dst = iota((narrow, wide), 0), iota((narrow, wide), 1)
    return jnp.where((dst // 2 == src) & (dst < valid), 1.0, 0.0).astype(F32)


def spread_left(wide, narrow):
    dst, src = iota((wide, narrow), 0), iota((wide, narrow), 1)
    return jnp.where(dst // 2 == src, 1.0, 0.0).astype(F32)


def plane_faces(e, spacing):
    rows, cols = e.shape
    x, y = iota(e.shape, 0), iota(e.shape, 1)
    fx = jnp.where(x > 0, face(e, back(e, 0), spacing), 0.0)
    fy = jnp.where(y > 0, face(e, back(e, 1), spacing), 0.0)
    edges = (jnp.where((x == 0) | (x == rows - 1), 1.0, 0.0)
             + jnp.where((y == 0) | (y == cols - 1), 1.0, 0.0))
    total = fx + ahead(fx, 0) + fy + ahead(fy, 1) + edges * e * (1.0 / spacing)
    return fx, fy, total


def plane_sum(fx, fy, v):
    return fx * back(v, 0) + ahead(fx * v, 0) + fy * back(v, 1) + ahead(fy * v, 1)


def coarse_cycle(e, k, planes, nx, sz, sx):
    rows = e.shape[0]
    row, lane = iota(e.shape, 0), iota(e.shape, 1)
    x, z = row % nx, row // nx
    valid = (row < planes * nx) & (lane < nx)
    e = jnp.where(valid, e, 1.0)
    fx = jnp.where(valid & (x > 0), face(e, back(e, 0), sx), 0.0) if nx > 1 else None
    fy = jnp.where(valid & (lane > 0), face(e, back(e, 1), sx), 0.0) if nx > 1 else None
    wrap = nx % rows
    fz = jnp.where(valid & (z > 0), face(e, back(e, 0, wrap), sz), 0.0) if planes > 1 else None
    diag = k + e * (
        (jnp.where(x == 0, 1.0, 0.0) + jnp.where(x == nx - 1, 1.0, 0.0)
         + jnp.where(lane == 0, 1.0, 0.0) + jnp.where(lane == nx - 1, 1.0, 0.0)) * (1.0 / sx)
        + (jnp.where(z == 0, 1.0, 0.0) + jnp.where(z == planes - 1, 1.0, 0.0)) * (1.0 / sz))
    if nx > 1:
        diag = diag + fx + ahead(fx, 0) + fy + ahead(fy, 1)
    if planes > 1:
        diag = diag + fz + ahead(fz, 0, wrap)
    w = jnp.where(valid, DAMPING / jnp.where(valid, diag, 1.0), 0.0)

    def beside(v):
        total = jnp.zeros_like(v)
        if nx > 1:
            total = plane_sum(fx, fy, v)
        if planes > 1:
            total = total + fz * back(v, 0, wrap) + ahead(fz * v, 0, wrap)
        return total

    def sweep(v, b):
        return (1.0 - DAMPING) * v + w * (b + beside(v))

    def coarsest(b):
        v = w * b
        for _ in range(COARSE_SWEEPS - 1):
            v = sweep(v, b)
        return v

    if planes == 1:
        return coarsest
    halve = nx > 1 and nx % 2 == 0
    nx2 = nx // 2 if halve else nx
    sx2 = sx * 4.0 if halve else sx
    step = planes
    while step * nx > 512 and step % 4 == 0:
        step //= 2
    part = step * nx
    if step == planes:
        part = rows
    real2 = planes // 2 * nx2
    rows2 = max(8, real2)
    part2 = rows2 if step == planes else step // 2 * nx2
    ratio = 2 if halve else 1

    def member(fine, coarse):
        return ((fine < step * nx) & ((fine // nx // 2) * nx2 + fine % nx // ratio == coarse))

    down = jnp.where(member(iota((part2, part), 1), iota((part2, part), 0)), 1.0, 0.0)
    up = jnp.where(member(iota((part, part2), 0), iota((part, part2), 1)), 1.0, 0.0)
    if halve:
        right = pool_right(LANES, LANES, nx)
        left = spread_right(LANES, LANES, nx)
        scale = 0.125
    else:
        scale = 0.5

    def coarsen(f):
        if halve:
            f = times(f, right)
        parts = [dot(down, f[i:i + part]) for i in range(0, rows, part)]
        return scale * (parts[0] if len(parts) == 1 else jnp.concatenate(parts, axis=0))

    def refine(f):
        if halve:
            f = times(f, left)
        parts = [dot(up, f[i:i + part2]) for i in range(0, rows2, part2)]
        return parts[0] if len(parts) == 1 else jnp.concatenate(parts, axis=0)

    below = coarse_cycle(coarsen(jnp.where(valid, e, 0.0)), coarsen(k),
                         planes // 2, nx2, sz * 4.0, sx2)

    def run(b):
        v = w * b
        for _ in range(PRE_SWEEPS - 1):
            v = sweep(v, b)
        r = jnp.where(valid, b - diag * v + beside(v), 0.0)
        v = v + refine(below(coarsen(r)))
        for _ in range(POST_SWEEPS):
            v = sweep(v, b)
        return v

    return run


REG, V0, V1, V2, BASE, FAR = range(6)
E1, A1, A2, A3, A4, TERM = range(6)


def kernel(n, partials, regions, previous, out,
           dens, got, b0, fx0, fy0, fz0, dg0, wt0, halo_reg, far_reg, fxh, fyh, fzh, wth, halo0, v1, v2, base,
           halo1, plane1, term1, gb, gk,
           big_send, big_recv, small_send, small_recv, many_send, many_recv, c2_planes):
    me = lax.axis_index("slab")
    job = lax.axis_index("job")
    nxy = regions.shape[1]
    half = nxy // 2
    quarter = nxy // 4
    rows = partials.shape[2]
    has_lo, has_hi = me > 0, me < n - 1

    def peer(index):
        return {"slab": index}

    barrier = pltpu.get_barrier_semaphore()

    def greet(off, carry):
        pl.semaphore_signal(barrier, inc=1, device_id=peer(lax.rem(me + off, n)),
                            device_id_type=pl.DeviceIdType.MESH)
        return carry

    lax.fori_loop(1, n, greet, 0)

    @pl.when(jnp.logical_not(has_lo))
    def _():
        for i in range(4):
            halo0[i, 0] = jnp.zeros((nxy, nxy), F32)
        for i in range(6):
            halo1[i, 0] = jnp.zeros((half, half), F32)
        halo_reg[0] = jnp.zeros((nxy, nxy), jnp.int32)
        far_reg[0] = jnp.zeros((nxy, nxy), jnp.int32)

    @pl.when(jnp.logical_not(has_hi))
    def _():
        for i in range(4):
            halo0[i, 1] = jnp.zeros((nxy, nxy), F32)
        for i in range(6):
            halo1[i, 1] = jnp.zeros((half, half), F32)
        halo_reg[1] = jnp.zeros((nxy, nxy), jnp.int32)
        far_reg[1] = jnp.zeros((nxy, nxy), jnp.int32)

    density = partials[0].astype(F32)
    for g in range(1, partials.shape[0]):
        density = density + partials[g].astype(F32)
    dens[...] = (SOURCE * density).reshape(dens.shape)

    pl.semaphore_wait(barrier, n - 1)

    def copies(first, last, dst, sends, recvs, i):
        to_lo = pltpu.make_async_remote_copy(
            src_ref=first, dst_ref=dst.at[1], send_sem=sends.at[i, 0], recv_sem=recvs.at[i, 1],
            device_id=peer(jnp.maximum(me - 1, 0)), device_id_type=pl.DeviceIdType.MESH)
        to_hi = pltpu.make_async_remote_copy(
            src_ref=last, dst_ref=dst.at[0], send_sem=sends.at[i, 1], recv_sem=recvs.at[i, 0],
            device_id=peer(jnp.minimum(me + 1, n - 1)), device_id_type=pl.DeviceIdType.MESH)

        def start():
            pl.when(has_lo)(to_lo.start)
            pl.when(has_hi)(to_hi.start)

        def recv():
            pl.when(has_lo)(to_hi.wait_recv)
            pl.when(has_hi)(to_lo.wait_recv)

        def sent():
            pl.when(has_lo)(to_lo.wait_send)
            pl.when(has_hi)(to_hi.wait_send)

        return start, recv, sent

    pending = []

    def launch(first, last, dst, sends, recvs, i):
        start, recv, sent = copies(first, last, dst, sends, recvs, i)
        start()
        pending.append(sent)
        return recv

    recv_reg = launch(regions.at[0], regions.at[1], halo_reg, big_send, big_recv, REG)
    recv_v0 = launch(previous.at[0], previous.at[1], halo0.at[0], big_send, big_recv, V0)

    def scatter(step, carry):
        other = lax.rem(me + 1 + lax.rem(step + n // 2 - 1, n - 1), n)
        pltpu.make_async_remote_copy(
            src_ref=dens.at[other], dst_ref=got.at[me], send_sem=many_send.at[0],
            recv_sem=many_recv.at[0], device_id=peer(other),
            device_id_type=pl.DeviceIdType.MESH).start()
        return carry

    lax.fori_loop(0, n - 1, scatter, 0)

    def dielectric(r):
        return jnp.where(r == 0, INSIDE, SOLVENT).astype(F32)

    e = [dielectric(regions[p]) for p in range(2)]
    k = [jnp.where(regions[p] == 2, SCREEN, 0.0).astype(F32) for p in range(2)]
    right0, left0 = pool_right(nxy, half, nxy), pool_left(half, nxy)
    right1, left1 = pool_right(half, LANES, half), pool_left(quarter, half)

    def down0(a, b):
        return 0.125 * dot(left0, times(a + b, right0))

    def down1(a):
        return 0.25 * dot(left1, times(a, right1))

    e1, k1 = down0(e[0], e[1]), down0(k[0], k[1])
    plane1[E1] = e1
    recv_e1 = launch(plane1.at[E1], plane1.at[E1], halo1.at[E1], small_send, small_recv, E1)
    core, chip = lax.rem(me, 2), me // 2
    gk[core, chip] = down1(e1) + back(down1(k1), 1, LANES // 2)

    def share(ref, i):
        def one(off, carry):
            other = lax.rem(me + 2 * off, n)
            pltpu.make_async_remote_copy(
                src_ref=ref.at[core, chip], dst_ref=ref.at[core, chip], send_sem=many_send.at[i],
                recv_sem=many_recv.at[i], device_id=peer(other),
                device_id_type=pl.DeviceIdType.MESH).start()
            return carry

        lax.fori_loop(1, n // 2, one, 0)

    def relay(ref, i):
        window = ref.at[0, pl.ds(0, n // 2 - 1)]
        pltpu.make_async_copy(window, window, many_recv.at[i]).wait()
        copy = pltpu.make_async_remote_copy(
            src_ref=ref.at[core], dst_ref=ref.at[core], send_sem=many_send.at[i + 2],
            recv_sem=many_recv.at[i + 2], device_id=peer(me + 1 - 2 * core),
            device_id_type=pl.DeviceIdType.MESH)
        copy.start()
        pending.append(pltpu.make_async_copy(window, window, many_send.at[i]).wait)
        pending.append(copy.wait_send)
        return copy.wait_recv

    def all_in(ref, sems, i):
        window = ref.at[pl.ds(0, n - 1)]
        pltpu.make_async_copy(window, window, sems.at[i]).wait()

    share(gk, 1)

    totals = []
    middle = face(e[0], e[1], 1.0)
    fz0[1] = middle
    part = []
    for p in range(2):
        fx, fy, total = plane_faces(e[p], 1.0)
        fx0[p] = fx
        fy0[p] = fy
        totals.append(total + middle + k[p])
        part.append(plane_sum(fx, fy, previous[p]) + middle * previous[1 - p])
    recv_reg()
    e_side = [jnp.where(has_lo, dielectric(halo_reg[0]), e[0]),
              jnp.where(has_hi, dielectric(halo_reg[1]), e[1])]
    for p in range(2):
        outer = face(e_side[p], e[p], 1.0)
        fz0[2 * p] = outer
        total = totals[p] + outer
        dg0[p] = total
        wt0[p] = DAMPING / total

    def beside0(p, mine, below, above):
        return plane_sum(fx0[p], fy0[p], mine) + fz0[p] * below + fz0[p + 1] * above

    def sweep0(p, mine, below, above):
        return (1.0 - DAMPING) * mine + wt0[p] * (b0[p] + beside0(p, mine, below, above))

    recv_v0()
    for p in range(2):
        v1[p] = (1.0 - DAMPING) * previous[p] + wt0[p] * (part[p] + fz0[2 * p] * halo0[0, p])

    got[me] = dens[me]
    all_in(got, many_recv, 0)
    for p in range(2):
        if rows % 8 == 0:
            b0[p] = got[:, p].reshape(nxy, nxy)
        else:
            for s in range(n):
                b0[p, s * rows:(s + 1) * rows, :] = got[s, p]
    for p in range(2):
        v1[p] = v1[p] + wt0[p] * b0[p]
    recv = launch(v1.at[0], v1.at[1], halo0.at[1], big_send, big_recv, V1)
    recv_gk = relay(gk, 1)
    recv_e1()
    sz1 = sx1 = 4.0
    fx1, fy1, total1 = plane_faces(e1, sx1)
    fz1lo = face(jnp.where(has_lo, halo1[E1, 0], e1), e1, sz1)
    fz1hi = face(jnp.where(has_hi, halo1[E1, 1], e1), e1, sz1)
    dg1 = total1 + fz1lo + fz1hi + k1
    wt1 = DAMPING / dg1

    recv()
    v2[0] = sweep0(0, v1[0], halo0[1, 0], v1[1])
    v2[1] = sweep0(1, v1[1], v1[0], halo0[1, 1])
    term1[0] = 0.125 * dot(left0, times(fz0[0] * v2[0], right0))
    term1[1] = 0.125 * dot(left0, times(fz0[2] * v2[1], right0))
    recv_term = launch(term1.at[0], term1.at[1], halo1.at[TERM], small_send, small_recv, TERM)
    recv_v2 = launch(v2.at[0], v2.at[1], halo0.at[2], big_send, big_recv, V2)
    r0 = b0[0] - dg0[0] * v2[0] + plane_sum(fx0[0], fy0[0], v2[0]) + fz0[1] * v2[1]
    r1 = b0[1] - dg0[1] * v2[1] + plane_sum(fx0[1], fy0[1], v2[1]) + fz0[1] * v2[0]
    b1 = down0(r0, r1)
    recv_far = launch(regions.at[1], regions.at[0], far_reg, big_send, big_recv, FAR)
    recv_gk()
    e2 = 0.5 * (gk[0] + gk[1]).reshape(n // 2 * quarter, LANES)
    k2 = back(e2, 1, LANES // 2)
    coarse = coarse_cycle(e2, k2, n // 2, quarter, 16.0, 16.0)
    recv_term()
    b1 = b1 + halo1[TERM, 0] + halo1[TERM, 1]

    def beside1(mine, i):
        return plane_sum(fx1, fy1, mine) + fz1lo * halo1[i, 0] + fz1hi * halo1[i, 1]

    def trade1(value, i):
        plane1[i] = value
        launch(plane1.at[i], plane1.at[i], halo1.at[i], small_send, small_recv, i)()

    a = wt1 * b1
    trade1(a, A1)
    a = (1.0 - DAMPING) * a + wt1 * (b1 + beside1(a, A1))
    trade1(a, A2)
    full = down1(b1 - dg1 * a + beside1(a, A2))
    gb[core, chip] = full[:quarter // 2] + back(full[quarter // 2:], 1, LANES // 2)
    share(gb, 2)
    recv_v2()
    base[0] = sweep0(0, v2[0], halo0[2, 0], v2[1])
    base[1] = sweep0(1, v2[1], v2[0], halo0[2, 1])
    recv_base = launch(base.at[0], base.at[1], halo0.at[3], big_send, big_recv, BASE)
    relay_gb = relay(gb, 2)
    recv_far()
    for p in range(2):
        region = halo_reg[p]
        beyond = face(e_side[p], dielectric(far_reg[p]), 1.0)
        fx, fy, total = plane_faces(e_side[p], 1.0)
        fxh[p] = fx
        fyh[p] = fy
        fzh[p] = beyond
        wth[p] = DAMPING / (total + beyond + fz0[2 * p] + jnp.where(region == 2, SCREEN, 0.0))
    relay_gb()
    packed = 0.5 * (gb[0] + gb[1]).reshape(n // 2 * quarter // 2, LANES)
    split = (n // 2, quarter // 2, LANES)
    b2 = jnp.concatenate(
        [packed.reshape(split), back(packed, 1, LANES // 2).reshape(split)], axis=1
    ).reshape(n // 2 * quarter, LANES)
    c2 = coarse(b2)

    for i in range(n // 2):
        c2_planes[i] = c2[i * quarter:(i + 1) * quarter]
    grow_l, grow_r = spread_left(half, quarter), spread_right(LANES, half, half)

    def up1(index):
        return dot(grow_l, times(c2_planes[index // 2], grow_r))

    halo1[A2, 0] = halo1[A2, 0] + jnp.where(has_lo, up1(jnp.maximum(me - 1, 0)), 0.0)
    halo1[A2, 1] = halo1[A2, 1] + jnp.where(has_hi, up1(jnp.minimum(me + 1, n - 1)), 0.0)
    a = a + up1(me)
    a = (1.0 - DAMPING) * a + wt1 * (b1 + beside1(a, A2))
    trade1(a, A3)
    a = (1.0 - DAMPING) * a + wt1 * (b1 + beside1(a, A3))
    trade1(a, A4)

    big_l, big_r = spread_left(nxy, half), spread_right(half, nxy, nxy)

    def up0(c):
        return dot(big_l, times(c, big_r))

    mine = up0(a)
    recv_base()
    v3, side = [], []
    present = [has_lo, has_hi]
    for p in range(2):
        c = up0(halo1[A4, p])
        own = plane_sum(fx0[p], fy0[p], mine) + fz0[1] * mine + fz0[2 * p] * c
        v3.append(base[p] + (1.0 - DAMPING) * mine + wt0[p] * own)
        other = plane_sum(fxh[p], fyh[p], c) + fzh[p] * c + fz0[2 * p] * mine
        swept = halo0[3, p] + (1.0 - DAMPING) * c + wth[p] * other
        side.append(jnp.where(present[p], swept, 0.0))
    out[0] = sweep0(0, v3[0], side[0], v3[1])
    out[1] = sweep0(1, v3[1], v3[0], side[1])

    for sent in pending:
        sent()
    all_in(got, many_send, 0)


def local(partials, regions, previous):
    n = lax.axis_size("slab")
    nxy = regions.shape[1]
    half, quarter = nxy // 2, nxy // 4
    rows = partials.shape[2]
    vmem = lambda *shape: pltpu.VMEM(shape, F32)
    spec = pl.BlockSpec(memory_space=pltpu.VMEM)
    return pl.pallas_call(
        functools.partial(kernel, n),
        out_shape=jax.ShapeDtypeStruct(previous.shape, F32),
        in_specs=[spec] * 3,
        out_specs=spec,
        scratch_shapes=[
            vmem(n, 2, rows, nxy), vmem(n, 2, rows, nxy), vmem(2, nxy, nxy),
            vmem(2, nxy, nxy), vmem(2, nxy, nxy), vmem(3, nxy, nxy), vmem(2, nxy, nxy),
            vmem(2, nxy, nxy),
            pltpu.VMEM((2, nxy, nxy), jnp.int32), pltpu.VMEM((2, nxy, nxy), jnp.int32),
            vmem(2, nxy, nxy), vmem(2, nxy, nxy), vmem(2, nxy, nxy), vmem(2, nxy, nxy),
            vmem(4, 2, nxy, nxy),
            vmem(2, nxy, nxy), vmem(2, nxy, nxy), vmem(2, nxy, nxy),
            vmem(6, 2, half, half), vmem(5, half, half), vmem(2, half, half),
            vmem(2, n // 2, quarter // 2, LANES), vmem(2, n // 2, quarter, LANES),
            pltpu.SemaphoreType.DMA((6, 2)), pltpu.SemaphoreType.DMA((6, 2)),
            pltpu.SemaphoreType.DMA((6, 2)), pltpu.SemaphoreType.DMA((6, 2)),
            pltpu.SemaphoreType.DMA((5,)), pltpu.SemaphoreType.DMA((5,)),
            vmem(n // 2, quarter, LANES),
        ],
        compiler_params=pltpu.CompilerParams(
            collective_id=0, has_side_effects=True, vmem_limit_bytes=60 * 1024 * 1024),
    )(partials, regions, previous)


def solution(mesh):
    in_specs = (
        P("job", None, "slab", None),
        P(("job", "slab"), None, None),
        P(("job", "slab"), None, None),
    )
    out_specs = P(("job", "slab"), None, None)
    return jax.shard_map(local, mesh=mesh, in_specs=in_specs, out_specs=out_specs, check_vma=False)
```
